32 devices in a mesh: mesh: 2 (over core), dom: 16 (over z, y, x).
Axes of the slice: x: 2, y: 2, z: 4, core: 2. Of those that a mesh axis runs over, the one named last changes fastest.
Arguments:
- donor_fields: float32 [5, 512, 4096], P(None, None, ('mesh', 'dom')), may hold values from -6 to 6
- interp_weights: float32 [3, 8, 65536], P(None, None, ('mesh', 'dom')), may hold values from -1 to 1, as said below
- donor_owner: int32 [65536, 1], P(('mesh', 'dom')), may hold values from 0 to 15, as said below
- donor_element: int32 [65536], P(('mesh', 'dom')), may hold values from 0 to 127
- geometry: float32 [4, 4096], P(None, ('mesh', 'dom')), may hold values from 0.25 to 4
- wall_flag: int32 [2, 256], P(None, ('mesh', 'dom')), may hold values 0 or 1
- forcing: float32 [512, 4096], P(None, ('mesh', 'dom')), may hold values from -6 to 6
Outputs:
- velocity: float32 [512, 4096], P(None, ('mesh', 'dom'))
- residual: float32 [512, 4096], P(None, ('mesh', 'dom'))
- interface_values: float32 [5, 65536], P(None, ('mesh', 'dom'))
The draws below stay inside these ranges and needn't reach their ends.
Inputs may be any that keep to these rules, and one draw needn't show every extreme that they name: `interp_weights`: for each receptor and direction, the 8 entries are the Lagrange polynomials of the order-7 Gauss-Lobatto-Legendre points evaluated at one point of [-1, 1]. `donor_owner`: the receptors of block q of a mesh (the rows of one device) name donor dom indices from q - 2 to q + 2 only; among them one index is named exactly 1024 times and no index more often.
All inputs are finite; a program needn't handle non-finite values. No bound on the sum of `wall_flag` on one device may be relied on, other than what follows from the above.
Results may differ from the reference program's by a relative error of at most 0.00026.
Values sent between devices are 32-bit elements; how exact they have to be, the bound alone decides.
A program may use at most 192 MiB of HBM per device.

```python
import math
import jax
import jax.numpy as jnp
import numpy as np
from jax import lax

FIELDS = 5
EX = 8
EY = 16
EZ_DEV = 1
ITERS = 3
PTS = 512
E_DEV = 128
E_TOTAL = 4096
R_DEV = 2048
R_TOTAL = 65536
CAP = 1024
W_TOTAL = 256
N_MESH = 2
N_DOM = 16


def legendre_pair_drawn(values, degree):
    previous = values * 0.0 + 1.0
    current = values * 1.0
    for poly_order in range(2, degree + 1):
        previous, current = (current, ((2 * poly_order - 1) * values * current - (poly_order - 1) * previous) / poly_order)
    return (current, previous)


def gll_abscissae():
    degree = 7
    points_count = degree + 1
    abscissae = np.cos(np.pi * np.arange(points_count) / degree)
    for newton_turn in range(80):
        top_poly, lower_poly = legendre_pair_drawn(abscissae, degree)
        abscissae = abscissae - (abscissae * top_poly - lower_poly) / (points_count * top_poly)
    return np.sort(abscissae)


def draw_interp_weights(key, part):
    abscissae = gll_abscissae()
    location = jax.random.uniform(key, (3, R_TOTAL), jnp.float32, -1.0, 1.0)
    basis_rows = []
    for node_index in range(8):
        product = jnp.ones_like(location)
        for partner in range(8):
            if partner != node_index:
                product = product * (location - abscissae[partner]) / (abscissae[node_index] - abscissae[partner])
        basis_rows.append(product)
    return jnp.stack(basis_rows, 1).astype(jnp.float32)


def draw_donor_owner(key, part):
    block_count = N_MESH * N_DOM
    slab_index = jnp.arange(block_count, dtype=jnp.int32) % N_DOM
    lowest = jnp.maximum(slab_index - 2, 0)
    highest = jnp.minimum(slab_index + 2, N_DOM - 1)
    window = highest - lowest + 1
    hot_owner = lowest + jax.random.randint(jax.random.fold_in(key, 11), (block_count,), 0, window)
    picks = jax.random.randint(jax.random.fold_in(key, 13), (block_count, R_DEV), 0, (window - 1)[:, None])
    other_owner = lowest[:, None] + picks
    other_owner = other_owner + (other_owner >= hot_owner[:, None]).astype(jnp.int32)
    block_keys = jax.random.split(jax.random.fold_in(key, 17), block_count)
    ranks = jax.vmap(lambda one_key: jax.random.permutation(one_key, R_DEV))(block_keys)
    owner = jnp.where(ranks < CAP, hot_owner[:, None], other_owner)
    return owner.reshape(R_TOTAL, 1).astype(jnp.int32)


def place_ends(values, own_key, smallest, largest):
    index_at = [jax.random.randint(jax.random.fold_in(own_key, axis), (), 0, length) for axis, length in enumerate(values.shape)]
    main_axis = values.shape.index(max(values.shape))
    next_to = index_at[:main_axis] + [(index_at[main_axis] + 1) % values.shape[main_axis]] + index_at[main_axis + 1:]
    return values.at[tuple(index_at)].set(smallest).at[tuple(next_to)].set(largest)


def shard_levels(own_key, shape, pieces, least, top_value):
    loudness = 1.0
    for axis_at, blocks in pieces:
        draws = jax.random.uniform(jax.random.fold_in(jax.random.fold_in(own_key, 6), axis_at), (blocks,), jnp.float32, least / len(pieces), top_value / len(pieces))
        loudness = loudness * jnp.repeat(jnp.exp(draws), shape[axis_at] // blocks).reshape((-1,) + (1,) * (len(shape) - 1 - axis_at))
    return loudness


def noise(key, dims, deviation, bound, shards=(), kind=jnp.bfloat16):
    values = jax.random.normal(key, dims, jnp.float32) * deviation
    if len(shards) > 0:
        values = shard_levels(key, dims, shards, -0.22, 0.18) * values
    return jnp.clip(values, min=-bound, max=bound).astype(kind)


def setup_inputs(seed: int = 0) -> dict:
    seeds = jax.random.split(jax.random.key(seed), 8)
    donor_fields = noise(seeds[0], (FIELDS, PTS, E_TOTAL), 1.0, 6.0, ((2, 32),), jnp.float32)
    interp_weights = draw_interp_weights(jax.random.fold_in(seeds[7], 71), 0)
    donor_owner = draw_donor_owner(jax.random.fold_in(seeds[7], 71), 0)
    donor_element = place_ends(jax.random.randint(seeds[3], (R_TOTAL,), 0, E_DEV), jax.random.fold_in(seeds[3], 1), 0, E_DEV - 1).astype(jnp.int32)
    geometry = jnp.clip(jnp.exp(math.log(4.0) - 2.7725887 * jax.random.uniform(seeds[4], (4, E_TOTAL), jnp.float32) ** shard_levels(seeds[4], (4, E_TOTAL), ((1, 32),), -0.2, 0.2)), 0.25, 4.0)
    wall_flag = place_ends((jax.random.randint(seeds[5], (2, W_TOTAL), 0, 4) < 3).astype(jnp.int32), jax.random.fold_in(seeds[5], 1), 0, 1)
    forcing = noise(seeds[6], (PTS, E_TOTAL), 1.0, 6.0, ((1, 32),), jnp.float32)
    return {"donor_fields": donor_fields, "interp_weights": interp_weights, "donor_owner": donor_owner, "donor_element": donor_element, "geometry": geometry, "wall_flag": wall_flag, "forcing": forcing}


HIGHEST = lax.Precision.HIGHEST


def legendre_pair(values, degree):
    previous = values * 0.0 + 1.0
    current = values * 1.0
    for poly_order in range(2, degree + 1):
        previous, current = current, ((2 * poly_order - 1) * values * current - (poly_order - 1) * previous) / poly_order
    return current, previous


def gll_tables():
    degree = 7
    points_count = degree + 1
    abscissae = np.cos(np.pi * np.arange(points_count) / degree)
    for newton_turn in range(80):
        top_poly, lower_poly = legendre_pair(abscissae, degree)
        abscissae = abscissae - (abscissae * top_poly - lower_poly) / (points_count * top_poly)
    abscissae = np.sort(abscissae)
    top_poly, lower_poly = legendre_pair(abscissae, degree)
    quad_weights = 2.0 / (degree * points_count * top_poly * top_poly)
    identity_mat = np.eye(points_count)
    spacing = abscissae[:, None] - abscissae[None, :] + identity_mat
    derivative = (top_poly[:, None] / (top_poly[None, :] * spacing)) * (1.0 - identity_mat)
    derivative[0, 0] = -degree * points_count / 4.0
    derivative[degree, degree] = degree * points_count / 4.0
    return jnp.asarray(derivative, jnp.float32), jnp.asarray(quad_weights, jnp.float32)


def cube_weights(quad_weights):
    return quad_weights[:, None, None, None] * quad_weights[None, :, None, None] * quad_weights[None, None, :, None]


def local_operator(field_data, geometry, derivative, quad_weights):
    weights_cube = cube_weights(quad_weights)
    grad_x = jnp.einsum('ai,kjie->kjae', derivative, field_data, precision=HIGHEST)
    grad_y = jnp.einsum('aj,kjie->kaie', derivative, field_data, precision=HIGHEST)
    grad_z = jnp.einsum('ak,kjie->ajie', derivative, field_data, precision=HIGHEST)
    result = jnp.einsum('ai,kjae->kjie', derivative, grad_x * (weights_cube * geometry[0]), precision=HIGHEST)
    result = result + jnp.einsum('aj,kaie->kjie', derivative, grad_y * (weights_cube * geometry[1]), precision=HIGHEST)
    result = result + jnp.einsum('ak,ajie->kjie', derivative, grad_z * (weights_cube * geometry[2]), precision=HIGHEST)
    return result + (weights_cube * geometry[3]) * field_data


def local_diagonal(geometry, derivative, quad_weights):
    stiff_diag = jnp.sum(derivative * derivative * quad_weights[:, None], axis=0)
    along_x = (quad_weights[:, None, None] * quad_weights[None, :, None] * stiff_diag[None, None, :])[..., None]
    along_y = (quad_weights[:, None, None] * stiff_diag[None, :, None] * quad_weights[None, None, :])[..., None]
    along_z = (stiff_diag[:, None, None] * quad_weights[None, :, None] * quad_weights[None, None, :])[..., None]
    return along_x * geometry[0] + along_y * geometry[1] + along_z * geometry[2] + cube_weights(quad_weights) * geometry[3]


def direct_sum(field_data):
    paired = field_data[:, :, :, -1, :, :, :-1] + field_data[:, :, :, 0, :, :, 1:]
    field_data = field_data.at[:, :, :, -1, :, :, :-1].set(paired).at[:, :, :, 0, :, :, 1:].set(paired)
    paired = field_data[:, :, -1, :, :, :-1, :] + field_data[:, :, 0, :, :, 1:, :]
    field_data = field_data.at[:, :, -1, :, :, :-1, :].set(paired).at[:, :, 0, :, :, 1:, :].set(paired)
    paired = field_data[:, -1, :, :, :-1, :, :] + field_data[:, 0, :, :, 1:, :, :]
    field_data = field_data.at[:, -1, :, :, :-1, :, :].set(paired).at[:, 0, :, :, 1:, :, :].set(paired)
    return field_data


def reference(donor_fields, interp_weights, donor_owner, donor_element, geometry, wall_flag, forcing):
    derivative, quad_weights = gll_tables()
    elem_dev = EX * EY * EZ_DEV
    elem_mesh = elem_dev * N_DOM
    rec_mesh = R_DEV * N_DOM
    layers = EZ_DEV * N_DOM
    receptor_mesh = jnp.arange(R_TOTAL, dtype=jnp.int32) // rec_mesh
    target = ((1 - receptor_mesh) * elem_mesh + donor_owner[:, 0] * elem_dev + donor_element).astype(jnp.int32)
    blocks = N_MESH * N_DOM
    target_blocks = target.reshape(blocks, R_DEV)
    weight_blocks = jnp.transpose(interp_weights.reshape(3, 8, blocks, R_DEV), (2, 0, 1, 3))

    def evaluate(block_pair):
        target_row, weight_row = block_pair
        gathered = jnp.take(donor_fields, target_row, axis=2).reshape(FIELDS, 8, 8, 8, R_DEV)
        reduced = jnp.einsum('fkjib,ib->fkjb', gathered, weight_row[0], precision=HIGHEST)
        reduced = jnp.einsum('fkjb,jb->fkb', reduced, weight_row[1], precision=HIGHEST)
        return jnp.einsum('fkb,kb->fb', reduced, weight_row[2], precision=HIGHEST)

    evaluated = lax.map(evaluate, (target_blocks, weight_blocks))
    interface_values = jnp.transpose(evaluated, (1, 0, 2)).reshape(FIELDS, R_TOTAL)

    brick_shape = (8, 8, 8, layers, EY, EX)
    flat_shape = (8, 8, 8, elem_mesh)
    weights_cube = cube_weights(quad_weights)
    velocities = []
    residuals = []
    for mesh_index in range(N_MESH):
        first_column = mesh_index * elem_mesh
        mesh_geometry = geometry[:, first_column:first_column + elem_mesh]
        source = forcing[:, first_column:first_column + elem_mesh].reshape(flat_shape)
        received = interface_values[0, mesh_index * rec_mesh:(mesh_index + 1) * rec_mesh]
        received = received.reshape(N_DOM, 2, EZ_DEV, EY, 8, 8)
        side_values = jnp.transpose(received, (1, 4, 5, 0, 2, 3)).reshape(2, 8, 8, layers, EY)
        wall_bits = wall_flag[:, mesh_index * EX * layers:(mesh_index + 1) * EX * layers].reshape(2, layers, EX)
        wall_bits = wall_bits.astype(jnp.float32)
        zero_brick = jnp.zeros(brick_shape, jnp.float32)
        rec_value = zero_brick.at[:, :, 0, :, :, 0].set(side_values[0]).at[:, :, -1, :, :, -1].set(side_values[1])
        rec_mark = zero_brick.at[:, :, 0, :, :, 0].set(1.0).at[:, :, -1, :, :, -1].set(1.0)
        wall_low = jnp.broadcast_to(wall_bits[0], (8, 8, layers, EX))
        wall_high = jnp.broadcast_to(wall_bits[1], (8, 8, layers, EX))
        wall_mark = zero_brick.at[:, 0, :, :, 0, :].set(wall_low).at[:, -1, :, :, -1, :].set(wall_high)
        diag_brick = local_diagonal(mesh_geometry, derivative, quad_weights).reshape(brick_shape)
        unit_brick = jnp.ones(brick_shape, jnp.float32)
        summed = direct_sum(jnp.stack([rec_value, rec_mark, wall_mark, unit_brick, diag_brick], 0))
        summed = summed.reshape((5,) + flat_shape)
        free_mask = 1.0 - jnp.minimum(summed[1] + summed[2], 1.0)
        boundary = summed[0] / jnp.maximum(summed[1], 1.0)
        multiplicity = summed[3]
        inverse = free_mask / summed[4]

        def apply_operator(vector):
            local_term = local_operator(vector, mesh_geometry, derivative, quad_weights)
            return free_mask * direct_sum(local_term.reshape((1,) + brick_shape))[0].reshape(flat_shape)

        def inner(left, right):
            return jnp.sum(left * right / multiplicity)

        loaded = (weights_cube * mesh_geometry[3]) * source - local_operator(boundary, mesh_geometry, derivative, quad_weights)
        rhs = free_mask * direct_sum(loaded.reshape((1,) + brick_shape))[0].reshape(flat_shape)
        solution = jnp.zeros(flat_shape, jnp.float32)
        residual_now = rhs
        precond = inverse * residual_now
        direction = precond
        precond_norm = inner(residual_now, precond)
        for iteration in range(ITERS):
            operator_image = apply_operator(direction)
            step_length = precond_norm / inner(direction, operator_image)
            solution = solution + step_length * direction
            residual_now = residual_now - step_length * operator_image
            if iteration + 1 < ITERS:
                precond = inverse * residual_now
                norm_next = inner(residual_now, precond)
                direction = precond + (norm_next / precond_norm) * direction
                precond_norm = norm_next
        velocities.append((boundary + solution).reshape(PTS, elem_mesh))
        residuals.append(residual_now.reshape(PTS, elem_mesh))
    return jnp.concatenate(velocities, 1), jnp.concatenate(residuals, 1), interface_values
```

```python
import functools

import jax
import jax.numpy as jnp
import numpy as np
from jax import lax
from jax.experimental import pallas as pl
from jax.experimental.pallas import tpu as pltpu
from jax.sharding import PartitionSpec as P

EX = 8
EY = 16
ITERS = 3
REACH = 2
CHUNK = 256
ORDER = (0, 7, 1, 2, 3, 4, 5, 6)
MESH = pl.DeviceIdType.MESH


def legendre_pair(values, degree):
    previous = values * 0.0 + 1.0
    current = values * 1.0
    for poly_order in range(2, degree + 1):
        previous, current = (
            current,
            ((2 * poly_order - 1) * values * current - (poly_order - 1) * previous) / poly_order,
        )
    return (current, previous)


def gll_tables():
    degree = 7
    points_count = degree + 1
    abscissae = np.cos(np.pi * np.arange(points_count) / degree)
    for newton_turn in range(80):
        top_poly, lower_poly = legendre_pair(abscissae, degree)
        abscissae = abscissae - (abscissae * top_poly - lower_poly) / (points_count * top_poly)
    abscissae = np.sort(abscissae)
    top_poly, lower_poly = legendre_pair(abscissae, degree)
    quad_weights = 2.0 / (degree * points_count * top_poly * top_poly)
    identity_mat = np.eye(points_count)
    spacing = abscissae[:, None] - abscissae[None, :] + identity_mat
    derivative = top_poly[:, None] / (top_poly[None, :] * spacing) * (1.0 - identity_mat)
    derivative[0, 0] = -degree * points_count / 4.0
    derivative[degree, degree] = degree * points_count / 4.0
    return (abscissae, derivative, quad_weights)


def kernel(
    n,
    request_ref,
    donor_ref,
    geometry_ref,
    wall_ref,
    forcing_ref,
    along_y_ref,
    along_x_ref,
    plane_ref,
    place_ref,
    velocity_ref,
    residual_ref,
    interface_ref,
    split,
    asked,
    answer,
    answered,
    faces,
    halo,
    dots,
    all_dots,
    state,
    image,
    direction,
    direction_image,
    inverse,
    free,
    sharing,
    boundary,
    ask_send,
    ask_recv,
    reply_send,
    reply_recv,
    face_send,
    face_recv,
    dot_send,
    dot_recv,
):
    points, derivative, quad = gll_tables()
    stiff = (derivative.T * quad) @ derivative / quad[:, None]
    fields = donor_ref.shape[0]
    elems = donor_ref.shape[2]
    receptors = request_ref.shape[1]
    slots = 2 * REACH + 1
    mesh_id = lax.axis_index("mesh")
    slab = lax.axis_index("dom")
    other = 1 - mesh_id

    def inside(index):
        return jnp.logical_and(index >= 0, index < n)

    barrier = pltpu.get_barrier_semaphore()
    greeted = n - 1
    for step in range(1, n):
        pl.semaphore_signal(
            barrier, inc=1, device_id=(mesh_id, lax.rem(slab + step, n)), device_id_type=MESH
        )
    for shift in range(-REACH, REACH + 1):
        greeted = greeted + jnp.where(inside(slab + shift), 1, 0)

        @pl.when(inside(slab + shift))
        def _():
            pl.semaphore_signal(
                barrier, inc=1, device_id=(other, slab + shift), device_id_type=MESH
            )

    pl.semaphore_wait(barrier, greeted)

    def ask(shift):
        return pltpu.make_async_remote_copy(
            src_ref=request_ref,
            dst_ref=asked.at[shift + REACH],
            send_sem=ask_send.at[shift + REACH],
            recv_sem=ask_recv.at[shift + REACH],
            device_id=(other, lax.rem(slab + shift + n, n)),
            device_id_type=MESH,
        )

    def reply(shift):
        return pltpu.make_async_remote_copy(
            src_ref=answer.at[shift + REACH],
            dst_ref=answered.at[shift + REACH],
            send_sem=reply_send.at[shift + REACH],
            recv_sem=reply_recv.at[shift + REACH],
            device_id=(other, lax.rem(slab - shift + n, n)),
            device_id_type=MESH,
        )

    def face_copy(phase, up):
        step = 1 if up else n - 1
        return pltpu.make_async_remote_copy(
            src_ref=faces.at[phase, 1 if up else 0],
            dst_ref=halo.at[phase, 0 if up else 1],
            send_sem=face_send.at[phase, 1 if up else 0],
            recv_sem=face_recv.at[phase, 0 if up else 1],
            device_id=(mesh_id, lax.rem(slab + step, n)),
            device_id_type=MESH,
        )

    def send_faces(phase):
        @pl.when(slab < n - 1)
        def _():
            face_copy(phase, True).start()

        @pl.when(slab > 0)
        def _():
            face_copy(phase, False).start()

    def wait_faces(phase):
        @pl.when(slab > 0)
        def _():
            face_copy(phase, True).wait_recv()

        @pl.when(slab < n - 1)
        def _():
            face_copy(phase, False).wait_recv()

        @pl.when(slab < n - 1)
        def _():
            face_copy(phase, True).wait_send()

        @pl.when(slab > 0)
        def _():
            face_copy(phase, False).wait_send()

    def dot_copy(turn, step):
        return pltpu.make_async_remote_copy(
            src_ref=dots.at[turn],
            dst_ref=all_dots.at[turn, slab],
            send_sem=dot_send.at[turn, step],
            recv_sem=dot_recv.at[turn, step],
            device_id=(mesh_id, lax.rem(slab + step, n)),
            device_id_type=MESH,
        )

    for distance in range(REACH + 1):
        for shift in sorted({distance, -distance}):

            @pl.when(inside(slab + shift))
            def _():
                ask(shift).start()

    phases = halo.shape[0]
    blank = jnp.zeros(halo.shape[2:], jnp.float32)

    @pl.when(slab == 0)
    def _():
        for phase in range(phases):
            halo[phase, 0] = blank

    @pl.when(slab == n - 1)
    def _():
        for phase in range(phases):
            halo[phase, 1] = blank

    node = lax.broadcasted_iota(jnp.int32, (8, elems), 0)
    element = lax.broadcasted_iota(jnp.int32, (8, elems), 1)
    x_index = element % EX
    y_index = element // EX % EY

    def flag(condition):
        return jnp.where(condition, 1.0, 0.0)

    x_low = flag((node == 0) & (x_index > 0))
    x_high = flag((node == 7) & (x_index < EX - 1))
    y_low = flag(y_index > 0)
    y_high = flag(y_index < EY - 1)

    def plane_sum(tile):
        below = pltpu.roll(pltpu.roll(tile, 1, 1), 1, 2)
        above = pltpu.roll(pltpu.roll(tile, 7, 1), elems - 1, 2)
        tile = tile + below * x_low + above * x_high
        low = tile[0] + y_low * pltpu.roll(tile[7], EX, 1)
        high = tile[7] + y_high * pltpu.roll(tile[0], elems - EX, 1)
        return jnp.concatenate([low[None], tile[1:7], high[None]], 0)

    def weights(layer):
        return plane_ref[...] * float(quad[layer])

    g_x, g_y, g_z, g_m = [geometry_ref[d : d + 1, :] for d in range(4)]

    diag_plane = jnp.zeros((8, 8, elems), jnp.float32) + g_m
    diag_plane = diag_plane + g_x * along_x_ref[0]
    diag_plane = diag_plane + jnp.concatenate(
        [(g_y * float(stiff[j, j]) + jnp.zeros((8, elems), jnp.float32))[None] for j in range(8)], 0
    )
    for layer in ORDER:
        image[layer] = plane_sum(
            weights(layer) * (diag_plane + g_z * float(stiff[layer, layer]))
        )
    wall_low = flag(y_index == 0) * wall_ref[0:1, :]
    wall_high = flag(y_index == EY - 1) * wall_ref[1:2, :]
    nothing = jnp.zeros((6, 8, elems), jnp.float32)
    wall_plane = plane_sum(jnp.concatenate([wall_low[None], nothing, wall_high[None]], 0))
    faces[0, 0] = image[0]
    faces[0, 1] = image[7]
    faces[1, 0] = wall_plane
    faces[1, 1] = wall_plane
    send_faces(0)
    send_faces(1)

    donors = donor_ref[...].reshape(fields * 512, elems)
    coarse = donors.astype(jnp.bfloat16)
    split[:, :elems] = coarse
    split[:, elems:] = (donors - coarse.astype(jnp.float32)).astype(jnp.bfloat16)

    code = lax.broadcasted_iota(jnp.int32, (elems, CHUNK), 0) + slab * elems
    code = code.astype(jnp.float32)
    basis = lax.broadcasted_iota(jnp.int32, (8, CHUNK), 0)
    norms = [
        float(1.0 / np.prod([points[a] - points[b] for b in range(8) if b != a])) for a in range(8)
    ]
    scale = jnp.zeros((8, CHUNK), jnp.float32)
    for a in range(8):
        scale = jnp.where(basis == a, norms[a], scale)

    def lagrange(position):
        value = scale
        for b in range(8):
            value = value * jnp.where(basis == b, 1.0, position - float(points[b]))
        return value

    def serve(turn, carry):
        shift = ((turn + 1) // 2) * (2 * (turn % 2) - 1)

        @pl.when(inside(slab - shift))
        def _():
            ask(shift).wait_recv()

            def part(chunk, carry):
                block = asked[shift + REACH, :, pl.ds(pl.multiple_of(chunk * CHUNK, CHUNK), CHUNK)]
                chosen = jnp.where(block[3:4, :] == code, 1.0, 0.0).astype(jnp.bfloat16)
                chosen = jnp.concatenate([chosen, chosen], 0)
                w_x, w_y, w_z = [lagrange(block[d : d + 1, :]) for d in range(3)]
                found = jnp.dot(split[...], chosen, preferred_element_type=jnp.float32)
                for field in range(fields):
                    cube = found[field * 512 : (field + 1) * 512].reshape(8, 64, CHUNK)
                    total = cube[0] * w_z[0:1, :]
                    for k in range(1, 8):
                        total = total + cube[k] * w_z[k : k + 1, :]
                    total = total.reshape(8, 8, CHUNK)
                    line = total[0] * w_y[0:1, :]
                    for j in range(1, 8):
                        line = line + total[j] * w_y[j : j + 1, :]
                    answer[shift + REACH, field, pl.ds(chunk, 1), :] = jnp.sum(
                        line * w_x, axis=0, keepdims=True
                    )
                return carry

            lax.fori_loop(0, receptors // CHUNK, part, 0)
            reply(shift).start()

        return carry

    lax.fori_loop(0, slots, serve, 0)

    z_low = jnp.where(slab > 0, 2.0, 1.0)
    z_high = jnp.where(slab < n - 1, 2.0, 1.0)
    x_count = 1.0 + x_low + x_high
    y_count_low = 1.0 + y_low
    y_count_high = 1.0 + y_high
    plane_count = jnp.concatenate(
        [(x_count * y_count_low)[None]]
        + [x_count[None]] * 6
        + [(x_count * y_count_high)[None]],
        0,
    )
    mark = flag((node == 0) & (x_index == 0)) + flag((node == 7) & (x_index == EX - 1))
    wait_faces(0)
    wait_faces(1)
    image[0] = image[0] + halo[0, 0]
    image[7] = image[7] + halo[0, 1]
    for layer in range(8):
        count = plane_count
        walls = wall_plane
        if layer == 0:
            count = count * z_low
            walls = walls + halo[1, 0]
        if layer == 7:
            count = count * z_high
            walls = walls + halo[1, 1]
        open_part = 1.0 - jnp.minimum(mark * count + walls, 1.0)
        sharing[layer] = 1.0 / count
        free[layer] = open_part
        inverse[layer] = open_part / image[layer]

    interface_sum = jnp.zeros((fields, receptors // CHUNK, CHUNK), jnp.float32)
    for shift in range(-REACH, REACH + 1):

        @pl.when(jnp.logical_not(inside(slab + shift)))
        def _():
            answered[shift + REACH] = jnp.zeros(answered.shape[1:], jnp.float32)

        @pl.when(inside(slab + shift))
        def _():
            reply(shift).wait_recv()

    for shift in range(-REACH, REACH + 1):
        interface_sum = interface_sum + answered[shift + REACH]
    for chunk in range(receptors // CHUNK):
        interface_ref[:, chunk * CHUNK : (chunk + 1) * CHUNK] = interface_sum[:, chunk, :]

    rows = interface_sum[0]
    groups = CHUNK // 64
    rows = jnp.concatenate([rows[:, t * 64 : (t + 1) * 64] for t in range(groups)], 0)
    placed = lax.dot_general(
        rows,
        place_ref[...],
        (((0,), (0,)), ((), ())),
        precision=lax.Precision.HIGHEST,
        preferred_element_type=jnp.float32,
    ).reshape(8, 8, elems)
    for layer in ORDER:
        spread = jnp.concatenate(
            [(jnp.broadcast_to(placed[layer, j : j + 1, :], (8, elems)) * mark)[None] for j in range(8)],
            0,
        )
        boundary[layer] = plane_sum(spread)
        if layer == 7:
            faces[2, 0] = boundary[0]
            faces[2, 1] = boundary[7]
            send_faces(2)
    wait_faces(2)
    boundary[0] = boundary[0] + halo[2, 0]
    boundary[7] = boundary[7] + halo[2, 1]
    for layer in range(8):
        boundary[layer] = boundary[layer] * sharing[layer]

    def local_tile(source, layer):
        tile = source[layer]
        along_z = source[0] * float(stiff[layer, 0])
        for k in range(1, 8):
            along_z = along_z + source[k] * float(stiff[layer, k])
        along_y = along_y_ref[0] * tile[0:1]
        for j in range(1, 8):
            along_y = along_y + along_y_ref[j] * tile[j : j + 1]
        along_x = along_x_ref[0] * tile
        for step in range(1, 8):
            along_x = along_x + along_x_ref[step] * pltpu.roll(tile, step, 1)
        total = g_x * along_x + g_y * along_y + g_z * along_z + g_m * tile
        return weights(layer) * total

    for layer in ORDER:
        loaded = weights(layer) * g_m * forcing_ref[layer] - local_tile(boundary, layer)
        residual_ref[layer] = plane_sum(loaded)
        if layer == 7:
            faces[3, 0] = residual_ref[0]
            faces[3, 1] = residual_ref[7]
            send_faces(3)
    wait_faces(3)
    residual_ref[0] = residual_ref[0] + halo[3, 0]
    residual_ref[7] = residual_ref[7] + halo[3, 1]
    for layer in range(8):
        residual_ref[layer] = residual_ref[layer] * free[layer]
        velocity_ref[layer] = boundary[layer]
        direction[layer] = jnp.zeros((8, 8, elems), jnp.float32)
        direction_image[layer] = jnp.zeros((8, 8, elems), jnp.float32)

    def iterate(turn, carry):
        norm, length = carry
        phase = turn + 4
        norm_part = jnp.zeros((8, 8, elems), jnp.float32)
        for layer in range(8):
            state[layer] = inverse[layer] * residual_ref[layer]
            norm_part = norm_part + state[layer] * residual_ref[layer] * sharing[layer]
        curve_part = jnp.zeros((8, 8, elems), jnp.float32)
        for layer in ORDER:
            tile = local_tile(state, layer)
            curve_part = curve_part + tile * state[layer]
            image[layer] = plane_sum(tile)
            if layer == 7:
                faces[phase, 0] = image[0]
                faces[phase, 1] = image[7]
                send_faces(phase)
        dots[turn, 0:1, :] = jnp.sum(jnp.sum(norm_part, axis=0), axis=0, keepdims=True)
        dots[turn, 1:2, :] = jnp.sum(jnp.sum(curve_part, axis=0), axis=0, keepdims=True)
        for step in range(1, n):
            dot_copy(turn, step).start()
        all_dots[turn, slab] = dots[turn]
        wait_faces(phase)
        image[0] = image[0] + halo[phase, 0]
        image[7] = image[7] + halo[phase, 1]
        for step in range(1, n):
            dot_copy(turn, step).wait_recv()
        sums = jnp.sum(jnp.sum(all_dots[turn], axis=0), axis=1, keepdims=True)
        norm_next, curvature = sums[0:1, :], sums[1:2, :]
        ratio = jnp.where(turn == 0, 0.0, norm_next / norm)
        length = norm_next / (curvature - ratio * norm_next / length)
        for layer in range(8):
            toward = state[layer] + ratio * direction[layer]
            toward_image = free[layer] * image[layer] + ratio * direction_image[layer]
            direction[layer] = toward
            direction_image[layer] = toward_image
            velocity_ref[layer] = velocity_ref[layer] + length * toward
            residual_ref[layer] = residual_ref[layer] - length * toward_image
        for step in range(1, n):
            dot_copy(turn, step).wait_send()
        return norm_next, length

    one = jnp.ones((1, 1), jnp.float32)
    lax.fori_loop(0, ITERS, iterate, (one, one))

    for shift in range(-REACH, REACH + 1):

        @pl.when(inside(slab + shift))
        def _():
            ask(shift).wait_send()

        @pl.when(inside(slab - shift))
        def _():
            reply(shift).wait_send()


def body(n, donor_fields, interp_weights, donor_owner, donor_element, geometry, wall_flag, forcing):
    points, derivative, quad = gll_tables()
    stiff = (derivative.T * quad) @ derivative / quad[:, None]
    fields = donor_fields.shape[0]
    elems = geometry.shape[1]
    receptors = donor_element.shape[0]
    slots = 2 * REACH + 1
    nodes = jnp.asarray(points, jnp.float32)
    position = jnp.sum(interp_weights * nodes[None, :, None], axis=1)
    code = (donor_owner[:, 0] * elems + donor_element).astype(jnp.float32)
    request = jnp.concatenate([position, code[None, :]], 0)
    walls = jnp.tile(wall_flag.astype(jnp.float32), (1, elems // wall_flag.shape[1]))
    along_y = np.zeros((8, 8, 8, elems), np.float32) + stiff.T[:, :, None, None]
    along_x = np.zeros((8, 8, elems), np.float32)
    for step in range(8):
        for i in range(8):
            along_x[step, i] = stiff[i, (i - step) % 8]
    plane = np.zeros((8, 8, elems), np.float32) + (quad[:, None] * quad[None, :])[:, :, None]
    groups = CHUNK // 64
    count = receptors // CHUNK
    per_side = count // 2
    place = np.zeros((groups * count, elems), np.float32)
    for group in range(groups):
        for chunk in range(count):
            y = groups * (chunk % per_side) + group
            place[group * count + chunk, y * EX + (EX - 1) * (chunk // per_side)] = 1.0
    cube = (8, 8, 8, elems)
    phases = 4 + ITERS
    vmem = pl.BlockSpec(memory_space=pltpu.VMEM)
    velocity, residual, interface = pl.pallas_call(
        functools.partial(kernel, n),
        out_shape=(
            jax.ShapeDtypeStruct(cube, jnp.float32),
            jax.ShapeDtypeStruct(cube, jnp.float32),
            jax.ShapeDtypeStruct((fields, receptors), jnp.float32),
        ),
        in_specs=[vmem] * 9,
        out_specs=(vmem, vmem, vmem),
        scratch_shapes=[
            pltpu.VMEM((fields * 512, 2 * elems), jnp.bfloat16),
            pltpu.VMEM((slots, 4, receptors), jnp.float32),
            pltpu.VMEM((slots, fields, count, CHUNK), jnp.float32),
            pltpu.VMEM((slots, fields, count, CHUNK), jnp.float32),
            pltpu.VMEM((phases, 2, 8, 8, elems), jnp.float32),
            pltpu.VMEM((phases, 2, 8, 8, elems), jnp.float32),
            pltpu.VMEM((ITERS, 2, 128), jnp.float32),
            pltpu.VMEM((ITERS, n, 2, 128), jnp.float32),
        ]
        + [pltpu.VMEM(cube, jnp.float32)] * 8
        + [pltpu.SemaphoreType.DMA((slots,))] * 4
        + [pltpu.SemaphoreType.DMA((phases, 2))] * 2
        + [pltpu.SemaphoreType.DMA((ITERS, n))] * 2,
        compiler_params=pltpu.CompilerParams(
            collective_id=0, has_side_effects=True, vmem_limit_bytes=48 * 1024 * 1024
        ),
    )(
        request,
        donor_fields,
        geometry,
        walls,
        forcing.reshape(cube),
        jnp.asarray(along_y),
        jnp.asarray(along_x),
        jnp.asarray(plane),
        jnp.asarray(place),
    )
    return (velocity.reshape(512, elems), residual.reshape(512, elems), interface)


def solution(mesh):
    in_specs = (
        P(None, None, ("mesh", "dom")),
        P(None, None, ("mesh", "dom")),
        P(("mesh", "dom"), None),
        P(("mesh", "dom")),
        P(None, ("mesh", "dom")),
        P(None, ("mesh", "dom")),
        P(None, ("mesh", "dom")),
    )
    out_specs = (P(None, ("mesh", "dom")), P(None, ("mesh", "dom")), P(None, ("mesh", "dom")))
    return jax.shard_map(
        functools.partial(body, mesh.shape["dom"]),
        mesh=mesh,
        in_specs=in_specs,
        out_specs=out_specs,
        check_vma=False,
    )
```

```python
import functools

import jax
import jax.numpy as jnp
import numpy as np
from jax import lax
from jax.experimental import pallas as pl
from jax.experimental.pallas import tpu as pltpu
from jax.sharding import PartitionSpec as P

EX = 8
EY = 16
ITERS = 3
REACH = 2
CHUNK = 256
ORDER = (0, 7, 1, 2, 3, 4, 5, 6)
MESH = pl.DeviceIdType.MESH


def legendre_pair(values, degree):
    previous = values * 0.0 + 1.0
    current = values * 1.0
    for poly_order in range(2, degree + 1):
        previous, current = (
            current,
            ((2 * poly_order - 1) * values * current - (poly_order - 1) * previous) / poly_order,
        )
    return (current, previous)


def gll_tables():
    degree = 7
    points_count = degree + 1
    abscissae = np.cos(np.pi * np.arange(points_count) / degree)
    for newton_turn in range(80):
        top_poly, lower_poly = legendre_pair(abscissae, degree)
        abscissae = abscissae - (abscissae * top_poly - lower_poly) / (points_count * top_poly)
    abscissae = np.sort(abscissae)
    top_poly, lower_poly = legendre_pair(abscissae, degree)
    quad_weights = 2.0 / (degree * points_count * top_poly * top_poly)
    identity_mat = np.eye(points_count)
    spacing = abscissae[:, None] - abscissae[None, :] + identity_mat
    derivative = top_poly[:, None] / (top_poly[None, :] * spacing) * (1.0 - identity_mat)
    derivative[0, 0] = -degree * points_count / 4.0
    derivative[degree, degree] = degree * points_count / 4.0
    return (abscissae, derivative, quad_weights)


def kernel(
    n,
    request_ref,
    donor_hbm,
    geometry_ref,
    wall_ref,
    forcing_hbm,
    velocity_ref,
    residual_ref,
    interface_ref,
    donor_ref,
    forcing_ref,
    along_y_ref,
    along_x_ref,
    plane_ref,
    load_sem,
    split,
    asked,
    answer,
    answered,
    faces,
    halo,
    dots,
    all_dots,
    state,
    image,
    direction,
    direction_image,
    inverse,
    free,
    sharing,
    boundary,
    ask_send,
    ask_recv,
    reply_send,
    reply_recv,
    face_send,
    face_recv,
    dot_send,
    dot_recv,
):
    points, derivative, quad = gll_tables()
    stiff = (derivative.T * quad) @ derivative / quad[:, None]
    fields = donor_ref.shape[0]
    elems = donor_ref.shape[2]
    receptors = request_ref.shape[1]
    slots = 2 * REACH + 1
    mesh_id = lax.axis_index("mesh")
    slab = lax.axis_index("dom")
    other = 1 - mesh_id

    donor_load = pltpu.make_async_copy(donor_hbm, donor_ref, load_sem.at[0])
    forcing_load = pltpu.make_async_copy(forcing_hbm, forcing_ref, load_sem.at[1])
    donor_load.start()
    forcing_load.start()

    def inside(index):
        return jnp.logical_and(index >= 0, index < n)

    barrier = pltpu.get_barrier_semaphore()
    greeted = n - 1
    for step in range(1, n):
        pl.semaphore_signal(
            barrier, inc=1, device_id=(mesh_id, lax.rem(slab + step, n)), device_id_type=MESH
        )
    for shift in range(-REACH, REACH + 1):
        greeted = greeted + jnp.where(inside(slab + shift), 1, 0)

        @pl.when(inside(slab + shift))
        def _():
            pl.semaphore_signal(
                barrier, inc=1, device_id=(other, slab + shift), device_id_type=MESH
            )

    pl.semaphore_wait(barrier, greeted)

    def ask(shift):
        return pltpu.make_async_remote_copy(
            src_ref=request_ref,
            dst_ref=asked.at[shift + REACH],
            send_sem=ask_send.at[shift + REACH],
            recv_sem=ask_recv.at[shift + REACH],
            device_id=(other, lax.rem(slab + shift + n, n)),
            device_id_type=MESH,
        )

    def reply(shift):
        return pltpu.make_async_remote_copy(
            src_ref=answer.at[shift + REACH],
            dst_ref=answered.at[shift + REACH],
            send_sem=reply_send.at[shift + REACH],
            recv_sem=reply_recv.at[shift + REACH],
            device_id=(other, lax.rem(slab - shift + n, n)),
            device_id_type=MESH,
        )

    def face_copy(phase, up):
        step = 1 if up else n - 1
        return pltpu.make_async_remote_copy(
            src_ref=faces.at[phase, 1 if up else 0],
            dst_ref=halo.at[phase, 0 if up else 1],
            send_sem=face_send.at[phase, 1 if up else 0],
            recv_sem=face_recv.at[phase, 0 if up else 1],
            device_id=(mesh_id, lax.rem(slab + step, n)),
            device_id_type=MESH,
        )

    def send_faces(phase):
        @pl.when(slab < n - 1)
        def _():
            face_copy(phase, True).start()

        @pl.when(slab > 0)
        def _():
            face_copy(phase, False).start()

    def wait_faces(phase):
        @pl.when(slab > 0)
        def _():
            face_copy(phase, True).wait_recv()

        @pl.when(slab < n - 1)
        def _():
            face_copy(phase, False).wait_recv()

        @pl.when(slab < n - 1)
        def _():
            face_copy(phase, True).wait_send()

        @pl.when(slab > 0)
        def _():
            face_copy(phase, False).wait_send()

    def dot_copy(turn, step):
        return pltpu.make_async_remote_copy(
            src_ref=dots.at[turn],
            dst_ref=all_dots.at[turn, slab],
            send_sem=dot_send.at[turn, step],
            recv_sem=dot_recv.at[turn, step],
            device_id=(mesh_id, lax.rem(slab + step, n)),
            device_id_type=MESH,
        )

    for distance in range(REACH + 1):
        for shift in sorted({distance, -distance}):

            @pl.when(inside(slab + shift))
            def _():
                ask(shift).start()

    phases = halo.shape[0]
    blank = jnp.zeros(halo.shape[2:], jnp.float32)

    @pl.when(slab == 0)
    def _():
        for phase in range(phases):
            halo[phase, 0] = blank

    @pl.when(slab == n - 1)
    def _():
        for phase in range(phases):
            halo[phase, 1] = blank

    node = lax.broadcasted_iota(jnp.int32, (8, elems), 0)
    element = lax.broadcasted_iota(jnp.int32, (8, elems), 1)
    x_index = element % EX
    y_index = element // EX % EY

    across = jnp.zeros((8, elems), jnp.float32)
    for a in range(8):
        across = jnp.where(node == a, float(quad[a]), across)
    for j in range(8):
        plane_ref[j] = across * float(quad[j])
        for m in range(8):
            along_y_ref[m, j] = jnp.full((8, elems), float(stiff[j, m]), jnp.float32)
    for step in range(8):
        turned = jnp.zeros((8, elems), jnp.float32)
        for i in range(8):
            turned = jnp.where(node == i, float(stiff[i, (i - step) % 8]), turned)
        along_x_ref[step] = turned

    def flag(condition):
        return jnp.where(condition, 1.0, 0.0)

    x_low = flag((node == 0) & (x_index > 0))
    x_high = flag((node == 7) & (x_index < EX - 1))
    y_low = flag(y_index > 0)
    y_high = flag(y_index < EY - 1)

    def plane_sum(tile):
        below = pltpu.roll(pltpu.roll(tile, 1, 1), 1, 2)
        above = pltpu.roll(pltpu.roll(tile, 7, 1), elems - 1, 2)
        tile = tile + below * x_low + above * x_high
        low = tile[0] + y_low * pltpu.roll(tile[7], EX, 1)
        high = tile[7] + y_high * pltpu.roll(tile[0], elems - EX, 1)
        return jnp.concatenate([low[None], tile[1:7], high[None]], 0)

    def weights(layer):
        return plane_ref[...] * float(quad[layer])

    g_x, g_y, g_z, g_m = [geometry_ref[d : d + 1, :] for d in range(4)]

    diag_plane = jnp.zeros((8, 8, elems), jnp.float32) + g_m
    diag_plane = diag_plane + g_x * along_x_ref[0]
    diag_plane = diag_plane + jnp.concatenate(
        [(g_y * float(stiff[j, j]) + jnp.zeros((8, elems), jnp.float32))[None] for j in range(8)], 0
    )
    for layer in ORDER:
        image[layer] = plane_sum(
            weights(layer) * (diag_plane + g_z * float(stiff[layer, layer]))
        )
    wall_low = flag(y_index == 0) * wall_ref[0:1, :]
    wall_high = flag(y_index == EY - 1) * wall_ref[1:2, :]
    nothing = jnp.zeros((6, 8, elems), jnp.float32)
    wall_plane = plane_sum(jnp.concatenate([wall_low[None], nothing, wall_high[None]], 0))
    faces[0, 0] = image[0]
    faces[0, 1] = image[7]
    faces[1, 0] = wall_plane
    faces[1, 1] = wall_plane
    send_faces(0)
    send_faces(1)

    donor_load.wait()
    donors = donor_ref[...].reshape(fields * 512, elems)
    coarse = donors.astype(jnp.bfloat16)
    split[:, :elems] = coarse
    split[:, elems:] = (donors - coarse.astype(jnp.float32)).astype(jnp.bfloat16)

    code = lax.broadcasted_iota(jnp.int32, (elems, CHUNK), 0) + slab * elems
    code = code.astype(jnp.float32)
    basis = lax.broadcasted_iota(jnp.int32, (8, CHUNK), 0)
    norms = [
        float(1.0 / np.prod([points[a] - points[b] for b in range(8) if b != a])) for a in range(8)
    ]
    scale = jnp.zeros((8, CHUNK), jnp.float32)
    for a in range(8):
        scale = jnp.where(basis == a, norms[a], scale)

    def lagrange(position):
        value = scale
        for b in range(8):
            value = value * jnp.where(basis == b, 1.0, position - float(points[b]))
        return value

    def serve(turn, carry):
        shift = ((turn + 1) // 2) * (2 * (turn % 2) - 1)

        @pl.when(inside(slab - shift))
        def _():
            ask(shift).wait_recv()

            def part(chunk, carry):
                block = asked[shift + REACH, :, pl.ds(pl.multiple_of(chunk * CHUNK, CHUNK), CHUNK)]
                chosen = jnp.where(block[3:4, :] == code, 1.0, 0.0).astype(jnp.bfloat16)
                chosen = jnp.concatenate([chosen, chosen], 0)
                w_x, w_y, w_z = [lagrange(block[d : d + 1, :]) for d in range(3)]
                found = jnp.dot(split[...], chosen, preferred_element_type=jnp.float32)
                for field in range(fields):
                    cube = found[field * 512 : (field + 1) * 512].reshape(8, 64, CHUNK)
                    total = cube[0] * w_z[0:1, :]
                    for k in range(1, 8):
                        total = total + cube[k] * w_z[k : k + 1, :]
                    total = total.reshape(8, 8, CHUNK)
                    line = total[0] * w_y[0:1, :]
                    for j in range(1, 8):
                        line = line + total[j] * w_y[j : j + 1, :]
                    answer[shift + REACH, field, pl.ds(chunk, 1), :] = jnp.sum(
                        line * w_x, axis=0, keepdims=True
                    )
                return carry

            lax.fori_loop(0, receptors // CHUNK, part, 0)
            reply(shift).start()

        return carry

    lax.fori_loop(0, slots, serve, 0)

    z_low = jnp.where(slab > 0, 2.0, 1.0)
    z_high = jnp.where(slab < n - 1, 2.0, 1.0)
    x_count = 1.0 + x_low + x_high
    y_count_low = 1.0 + y_low
    y_count_high = 1.0 + y_high
    plane_count = jnp.concatenate(
        [(x_count * y_count_low)[None]]
        + [x_count[None]] * 6
        + [(x_count * y_count_high)[None]],
        0,
    )
    mark = flag((node == 0) & (x_index == 0)) + flag((node == 7) & (x_index == EX - 1))
    wait_faces(0)
    wait_faces(1)
    image[0] = image[0] + halo[0, 0]
    image[7] = image[7] + halo[0, 1]
    for layer in range(8):
        count = plane_count
        walls = wall_plane
        if layer == 0:
            count = count * z_low
            walls = walls + halo[1, 0]
        if layer == 7:
            count = count * z_high
            walls = walls + halo[1, 1]
        open_part = 1.0 - jnp.minimum(mark * count + walls, 1.0)
        sharing[layer] = 1.0 / count
        free[layer] = open_part
        inverse[layer] = open_part / image[layer]

    interface_sum = jnp.zeros((fields, receptors // CHUNK, CHUNK), jnp.float32)
    for shift in range(-REACH, REACH + 1):

        @pl.when(jnp.logical_not(inside(slab + shift)))
        def _():
            answered[shift + REACH] = jnp.zeros(answered.shape[1:], jnp.float32)

        @pl.when(inside(slab + shift))
        def _():
            reply(shift).wait_recv()

    for shift in range(-REACH, REACH + 1):
        interface_sum = interface_sum + answered[shift + REACH]
    for chunk in range(receptors // CHUNK):
        interface_ref[:, chunk * CHUNK : (chunk + 1) * CHUNK] = interface_sum[:, chunk, :]

    rows = interface_sum[0]
    groups = CHUNK // 64
    rows = jnp.concatenate([rows[:, t * 64 : (t + 1) * 64] for t in range(groups)], 0)
    count = receptors // CHUNK
    per_side = count // 2
    row = lax.broadcasted_iota(jnp.int32, (groups * count, elems), 0)
    spot = lax.broadcasted_iota(jnp.int32, (groups * count, elems), 1)
    piece = row % count
    target = (groups * (piece % per_side) + row // count) * EX + (EX - 1) * (piece // per_side)
    placed = lax.dot_general(
        rows,
        flag(spot == target),
        (((0,), (0,)), ((), ())),
        precision=lax.Precision.HIGHEST,
        preferred_element_type=jnp.float32,
    ).reshape(8, 8, elems)
    for layer in ORDER:
        spread = jnp.concatenate(
            [(jnp.broadcast_to(placed[layer, j : j + 1, :], (8, elems)) * mark)[None] for j in range(8)],
            0,
        )
        boundary[layer] = plane_sum(spread)
        if layer == 7:
            faces[2, 0] = boundary[0]
            faces[2, 1] = boundary[7]
            send_faces(2)
    wait_faces(2)
    boundary[0] = boundary[0] + halo[2, 0]
    boundary[7] = boundary[7] + halo[2, 1]
    for layer in range(8):
        boundary[layer] = boundary[layer] * sharing[layer]

    def local_tile(source, layer):
        tile = source[layer]
        along_z = source[0] * float(stiff[layer, 0])
        for k in range(1, 8):
            along_z = along_z + source[k] * float(stiff[layer, k])
        along_y = along_y_ref[0] * tile[0:1]
        for j in range(1, 8):
            along_y = along_y + along_y_ref[j] * tile[j : j + 1]
        along_x = along_x_ref[0] * tile
        for step in range(1, 8):
            along_x = along_x + along_x_ref[step] * pltpu.roll(tile, step, 1)
        total = g_x * along_x + g_y * along_y + g_z * along_z + g_m * tile
        return weights(layer) * total

    forcing_load.wait()
    for layer in ORDER:
        loaded = weights(layer) * g_m * forcing_ref[layer] - local_tile(boundary, layer)
        residual_ref[layer] = plane_sum(loaded)
        if layer == 7:
            faces[3, 0] = residual_ref[0]
            faces[3, 1] = residual_ref[7]
            send_faces(3)
    wait_faces(3)
    residual_ref[0] = residual_ref[0] + halo[3, 0]
    residual_ref[7] = residual_ref[7] + halo[3, 1]
    for layer in range(8):
        residual_ref[layer] = residual_ref[layer] * free[layer]
        velocity_ref[layer] = boundary[layer]
        direction[layer] = jnp.zeros((8, 8, elems), jnp.float32)
        direction_image[layer] = jnp.zeros((8, 8, elems), jnp.float32)

    def iterate(turn, carry):
        norm, length = carry
        phase = turn + 4
        norm_part = jnp.zeros((8, 8, elems), jnp.float32)
        for layer in range(8):
            state[layer] = inverse[layer] * residual_ref[layer]
            norm_part = norm_part + state[layer] * residual_ref[layer] * sharing[layer]
        curve_part = jnp.zeros((8, 8, elems), jnp.float32)
        for layer in ORDER:
            tile = local_tile(state, layer)
            curve_part = curve_part + tile * state[layer]
            image[layer] = plane_sum(tile)
            if layer == 7:
                faces[phase, 0] = image[0]
                faces[phase, 1] = image[7]
                send_faces(phase)
        dots[turn, 0:1, :] = jnp.sum(jnp.sum(norm_part, axis=0), axis=0, keepdims=True)
        dots[turn, 1:2, :] = jnp.sum(jnp.sum(curve_part, axis=0), axis=0, keepdims=True)
        for step in range(1, n):
            dot_copy(turn, step).start()
        all_dots[turn, slab] = dots[turn]
        wait_faces(phase)
        image[0] = image[0] + halo[phase, 0]
        image[7] = image[7] + halo[phase, 1]
        for step in range(1, n):
            dot_copy(turn, step).wait_recv()
        sums = jnp.sum(jnp.sum(all_dots[turn], axis=0), axis=1, keepdims=True)
        norm_next, curvature = sums[0:1, :], sums[1:2, :]
        ratio = jnp.where(turn == 0, 0.0, norm_next / norm)
        length = norm_next / (curvature - ratio * norm_next / length)
        for layer in range(8):
            toward = state[layer] + ratio * direction[layer]
            toward_image = free[layer] * image[layer] + ratio * direction_image[layer]
            direction[layer] = toward
            direction_image[layer] = toward_image
            velocity_ref[layer] = velocity_ref[layer] + length * toward
            residual_ref[layer] = residual_ref[layer] - length * toward_image
        for step in range(1, n):
            dot_copy(turn, step).wait_send()
        return norm_next, length

    one = jnp.ones((1, 1), jnp.float32)
    lax.fori_loop(0, ITERS, iterate, (one, one))

    for shift in range(-REACH, REACH + 1):

        @pl.when(inside(slab + shift))
        def _():
            ask(shift).wait_send()

        @pl.when(inside(slab - shift))
        def _():
            reply(shift).wait_send()


def body(n, donor_fields, interp_weights, donor_owner, donor_element, geometry, wall_flag, forcing):
    points, _, _ = gll_tables()
    fields = donor_fields.shape[0]
    elems = geometry.shape[1]
    receptors = donor_element.shape[0]
    slots = 2 * REACH + 1
    nodes = jnp.asarray(points, jnp.float32)
    position = jnp.sum(interp_weights * nodes[None, :, None], axis=1)
    code = (donor_owner[:, 0] * elems + donor_element).astype(jnp.float32)
    request = jnp.concatenate([position, code[None, :]], 0)
    walls = jnp.tile(wall_flag.astype(jnp.float32), (1, elems // wall_flag.shape[1]))
    count = receptors // CHUNK
    cube = (8, 8, 8, elems)
    phases = 4 + ITERS
    vmem = pl.BlockSpec(memory_space=pltpu.VMEM)
    hbm = pl.BlockSpec(memory_space=pl.ANY)
    velocity, residual, interface = pl.pallas_call(
        functools.partial(kernel, n),
        out_shape=(
            jax.ShapeDtypeStruct(cube, jnp.float32),
            jax.ShapeDtypeStruct(cube, jnp.float32),
            jax.ShapeDtypeStruct((fields, receptors), jnp.float32),
        ),
        in_specs=[vmem, hbm, vmem, vmem, hbm],
        out_specs=(vmem, vmem, vmem),
        scratch_shapes=[
            pltpu.VMEM((fields, 512, elems), jnp.float32),
            pltpu.VMEM(cube, jnp.float32),
            pltpu.VMEM(cube, jnp.float32),
            pltpu.VMEM((8, 8, elems), jnp.float32),
            pltpu.VMEM((8, 8, elems), jnp.float32),
            pltpu.SemaphoreType.DMA((2,)),
            pltpu.VMEM((fields * 512, 2 * elems), jnp.bfloat16),
            pltpu.VMEM((slots, 4, receptors), jnp.float32),
            pltpu.VMEM((slots, fields, count, CHUNK), jnp.float32),
            pltpu.VMEM((slots, fields, count, CHUNK), jnp.float32),
            pltpu.VMEM((phases, 2, 8, 8, elems), jnp.float32),
            pltpu.VMEM((phases, 2, 8, 8, elems), jnp.float32),
            pltpu.VMEM((ITERS, 2, 128), jnp.float32),
            pltpu.VMEM((ITERS, n, 2, 128), jnp.float32),
        ]
        + [pltpu.VMEM(cube, jnp.float32)] * 8
        + [pltpu.SemaphoreType.DMA((slots,))] * 4
        + [pltpu.SemaphoreType.DMA((phases, 2))] * 2
        + [pltpu.SemaphoreType.DMA((ITERS, n))] * 2,
        compiler_params=pltpu.CompilerParams(
            collective_id=0, has_side_effects=True, vmem_limit_bytes=48 * 1024 * 1024
        ),
    )(
        request,
        donor_fields,
        geometry,
        walls,
        forcing.reshape(cube),
    )
    return (velocity.reshape(512, elems), residual.reshape(512, elems), interface)


def solution(mesh):
    in_specs = (
        P(None, None, ("mesh", "dom")),
        P(None, None, ("mesh", "dom")),
        P(("mesh", "dom"), None),
        P(("mesh", "dom")),
        P(None, ("mesh", "dom")),
        P(None, ("mesh", "dom")),
        P(None, ("mesh", "dom")),
    )
    out_specs = (P(None, ("mesh", "dom")), P(None, ("mesh", "dom")), P(None, ("mesh", "dom")))
    return jax.shard_map(
        functools.partial(body, mesh.shape["dom"]),
        mesh=mesh,
        in_specs=in_specs,
        out_specs=out_specs,
        check_vma=False,
    )
```
